32 devices in a mesh: row: 4 (over y, x), col: 8 (over z, core).
Axes of the slice: x: 2, y: 2, z: 4, core: 2. Of those that a mesh axis runs over, the one named last changes fastest.
Arguments:
- wavefield: bfloat16 [2, 1, 8192, 8192], P(None, None, 'row', 'col'), as said below
- panel_order: int32 [16], replicated, may hold values from 0 to 15, each once
- filter_taps: float32 [11, 8192], P(None, 'col'), may hold values from -4 to 4
Outputs:
- primaries: bfloat16 [2, 1, 8192, 8192], P(None, None, 'row', 'col')
The draws below stay inside these ranges and needn't reach their ends.
Inputs may be any that keep to these rules, and one draw needn't show every extreme that they name: Reciprocity: wavefield[c, f, s, r] = wavefield[c, f, r, s] for every part, frequency, shot and receiver.
All inputs are finite; a program needn't handle non-finite values.
Results may differ from the reference program's by a relative error of at most 0.00045.
Values may be sent and summed in bfloat16 or wider, within the bound.
A program may use at most 128 MiB of HBM per device.

```python
import math
import jax
import jax.numpy as jnp
from jax import lax

SIDE = 8192
PANEL = 512
STEPS = 3
FREQ = 1
TAPS = 11
FIRST_FREQUENCY = 8
NT = 1024
NPANEL = 16


def draw_wavefield(key, part):
    first, second, third = jax.random.split(jax.random.fold_in(key, 17), 3)
    profile_key, phase_key = jax.random.split(third)
    position = jnp.arange(SIDE, dtype=jnp.float32) / SIDE
    jitter = jax.random.uniform(second, (SIDE,), jnp.float32)
    profile = jnp.clip(jax.random.normal(profile_key, (FREQ, SIDE), jnp.float32), -2.5, 2.5)
    angle = jax.random.uniform(phase_key, (FREQ,), jnp.float32, -3.14159265, 3.14159265)
    amplitude = 0.35 * jnp.stack([jnp.cos(angle), jnp.sin(angle)])
    base = jnp.clip(jax.random.normal(first, (2, FREQ, SIDE, SIDE), jnp.float32), -4.0, 4.0)
    weights = 10.0 ** (0.5 * position + 0.5 * jitter - 0.5)
    mirrored = (base + jnp.swapaxes(base, 2, 3)) * 0.70710678
    coherent = amplitude[:, :, None, None] * profile[None, :, :, None] * profile[None, :, None, :]
    mirrored = mirrored + coherent
    return (mirrored * weights[:, None] * weights[None, :]).astype(jnp.bfloat16)


def steps_of(rng, extent, cuts, smallest, largest):
    def one(axis_at, parts):
        heights = jax.random.uniform(jax.random.fold_in(jax.random.fold_in(rng, 6), axis_at), (parts,), jnp.float32, smallest / len(cuts), largest / len(cuts))
        return jnp.repeat(jnp.exp(heights), extent[axis_at] // parts).reshape((-1,) + (1,) * (len(extent) - axis_at - 1))

    level = one(*cuts[0])
    for cut in cuts[1:]:
        level = level * one(*cut)
    return level


def centred(rng, extent, spread, limit, shards=(), kind=jnp.bfloat16):
    values = spread * jax.random.normal(rng, extent, jnp.float32)
    if shards:
        values = values * steps_of(rng, extent, shards, -0.22, 0.18)
    return jnp.clip(values, -limit, limit).astype(kind)


def setup_inputs(seed: int = 0) -> dict:
    arg_keys = jax.random.split(jax.random.key(seed), 4)
    return {
        "wavefield": draw_wavefield(jax.random.fold_in(arg_keys[3], 71), 0),
        "panel_order": jax.random.permutation(arg_keys[1], NPANEL).astype(jnp.int32),
        "filter_taps": centred(arg_keys[2], (TAPS, SIDE), 0.3, 4.0, ((1, 8),), jnp.float32),
    }


def frequency_spectrum(filter_taps):
    lags = jnp.arange(TAPS, dtype=jnp.float32)
    omega = 2.0 * math.pi * (FIRST_FREQUENCY + jnp.arange(FREQ, dtype=jnp.float32)) / NT
    phase = omega[:, None] * lags[None, :]
    real_part = jnp.dot(jnp.cos(phase), filter_taps, precision=lax.Precision.HIGHEST)
    imag_part = -jnp.dot(jnp.sin(phase), filter_taps, precision=lax.Precision.HIGHEST)
    return (real_part, imag_part)

def reference(wavefield, panel_order, filter_taps):
    picks = (panel_order[:STEPS, None] * PANEL + jnp.arange(PANEL, dtype=jnp.int32)[None, :]).reshape(-1).astype(jnp.int32)
    spec_re, spectrum_imaginary = frequency_spectrum(filter_taps)
    factor = 1.0 / math.sqrt(STEPS * PANEL)
    count = 2.0 * SIDE * SIDE

    def one_slice(index):
        field = wavefield[:, index]
        upper = field[:, :, picks]
        lower = field[:, picks, :]
        left_factor = jnp.concatenate([upper[0], upper[1]], axis=1)
        right_factor = jnp.concatenate([jnp.concatenate([lower[0], lower[1]], axis=1), jnp.concatenate([-lower[1], lower[0]], axis=1)], axis=0)
        product = jnp.dot(left_factor, right_factor, preferred_element_type=jnp.float32) * factor
        mult_re = product[:, :SIDE]
        mult_im = product[:, SIDE:]
        energy_data = jnp.sum(jnp.square(field.astype(jnp.float32))) / count
        energy_mult = (jnp.sum(mult_re * mult_re) + jnp.sum(mult_im * mult_im)) / count
        gain = jnp.sqrt((energy_data + 1e-05) / (energy_mult + 1e-05))
        a_re = spec_re[index][None, :]
        a_im = spectrum_imaginary[index][None, :]
        sub_re = gain * (a_re * mult_re - a_im * mult_im)
        subtracted_imaginary = gain * (a_re * mult_im + a_im * mult_re)
        return jnp.stack([field[0].astype(jnp.float32) - sub_re, field[1].astype(jnp.float32) - subtracted_imaginary]).astype(jnp.bfloat16)
    result = lax.map(one_slice, jnp.arange(FREQ, dtype=jnp.int32))
    return jnp.swapaxes(result, 0, 1)
```

```python
import math

import jax
import jax.numpy as jnp
from jax import lax
from jax.experimental import pallas as pl
from jax.experimental.pallas import tpu as pltpu
from jax.sharding import PartitionSpec as P

SIDE = 8192
PANEL = 512
STEPS = 3
TAPS = 11
FIRST_FREQUENCY = 8
NT = 1024
MESH = pl.DeviceIdType.MESH

CHUNK = 64
NCHUNK = STEPS * PANEL // CHUNK
GROUP = 4
NGROUP = NCHUNK // GROUP
TILE = 256
LAG = 5


def spread(block, axis, holder):
    block = jnp.where(lax.axis_index(axis) == holder, block, jnp.zeros_like(block))
    return lax.psum(block, axis)


def frequency_spectrum(filter_taps, freq_count):
    lags = jnp.arange(TAPS, dtype=jnp.float32)
    omega = 2.0 * math.pi * (FIRST_FREQUENCY + jnp.arange(freq_count, dtype=jnp.float32)) / NT
    phase = omega[:, None] * lags[None, :]
    real_part = jnp.dot(jnp.cos(phase), filter_taps, precision=lax.Precision.HIGHEST)
    imag_part = -jnp.dot(jnp.sin(phase), filter_taps, precision=lax.Precision.HIGHEST)
    return (real_part, imag_part)


def local(wavefield, panel_order, filter_taps):
    freq_count = wavefield.shape[1]
    shot_block = wavefield.shape[2]
    recv_block = wavefield.shape[3]
    own_row_index = lax.axis_index("row")
    factor = 1.0 / math.sqrt(STEPS * PANEL)
    count = 2.0 * SIDE * SIDE
    local_data = jnp.sum(jnp.square(wavefield.astype(jnp.float32)), axis=(0, 2, 3))
    energy_data = lax.psum(local_data, ("row", "col"))
    totals = jnp.zeros((freq_count, shot_block, 2 * recv_block), jnp.float32)
    for panel_advance in range(STEPS):
        first_point = panel_order[panel_advance] * PANEL
        row_width = min(PANEL, shot_block)
        owner_turn = 0
        start = first_point + owner_turn * row_width
        piece = lax.dynamic_slice_in_dim(wavefield, start % shot_block, row_width, 2)
        row_pieces = spread(piece, "row", start // shot_block)
        col_pieces = []
        mirror_width = min(shot_block, recv_block)
        for owner_turn in range(max(1, shot_block // recv_block)):
            start = own_row_index * shot_block + owner_turn * mirror_width
            piece = row_pieces
            col_pieces.append(spread(piece, "col", start // recv_block))
        upper = jnp.swapaxes(jnp.concatenate(col_pieces, axis=3), 2, 3)
        left_factor = jnp.concatenate([upper[0], upper[1]], axis=2)
        right_factor = jnp.concatenate(
            [
                jnp.concatenate([row_pieces[0], row_pieces[1]], axis=2),
                jnp.concatenate([-row_pieces[1], row_pieces[0]], axis=2),
            ],
            axis=1,
        )
        totals = totals + jnp.einsum(
            "yga,yah->ygh", left_factor, right_factor, preferred_element_type=jnp.float32
        )
    mult_re = totals[:, :, :recv_block] * factor
    mult_im = totals[:, :, recv_block:] * factor
    local_mult = jnp.sum(mult_re * mult_re, axis=(1, 2)) + jnp.sum(mult_im * mult_im, axis=(1, 2))
    energy_mult = lax.psum(local_mult, ("row", "col"))
    gain = jnp.sqrt((energy_data / count + 1e-05) / (energy_mult / count + 1e-05))[:, None, None]
    spec_re, spectrum_imaginary = frequency_spectrum(filter_taps, freq_count)
    a_re = spec_re[:, None, :]
    a_im = spectrum_imaginary[:, None, :]
    sub_re = gain * (a_re * mult_re - a_im * mult_im)
    subtracted_imaginary = gain * (a_re * mult_im + a_im * mult_re)
    result = jnp.stack(
        [
            wavefield[0].astype(jnp.float32) - sub_re,
            wavefield[1].astype(jnp.float32) - subtracted_imaginary,
        ]
    )
    return result.astype(jnp.bfloat16)


def predict_kernel(pieces, mult, energy, own, first, second, left, acc, right,
                   xs, xr, ys, yr, us, ds, zr, ps, pr, own_sem, out_sem):
    row = lax.axis_index("row")
    col = lax.axis_index("col")
    z = col // 2
    core = col % 2
    along_x = row + 1 - 2 * (row % 2)
    along_y = (row + 2) % 4
    partner = col + 1 - 2 * core
    width = first.shape[3]
    above = z - row
    far = jnp.abs(above)

    load = pltpu.make_async_copy(pieces, own, own_sem)
    load.start()
    barrier = pltpu.get_barrier_semaphore()
    pl.semaphore_signal(barrier, inc=1, device_id=(along_x, col), device_id_type=MESH)
    pl.semaphore_signal(barrier, inc=1, device_id=(along_y, col), device_id_type=MESH)
    pl.semaphore_signal(barrier, inc=1, device_id=(row, partner), device_id_type=MESH)

    @pl.when(z > 0)
    def _():
        pl.semaphore_signal(barrier, inc=1, device_id=(row, col - 2), device_id_type=MESH)

    @pl.when(z < 3)
    def _():
        pl.semaphore_signal(barrier, inc=1, device_id=(row, col + 2), device_id_type=MESH)

    pl.semaphore_wait(barrier, 3 + jnp.minimum(z, 1) + jnp.minimum(3 - z, 1))

    def x_copy(k):
        to = along_x + (k % 2) * (along_y - along_x)
        return pltpu.make_async_remote_copy(
            src_ref=pieces.at[k], dst_ref=first.at[k], send_sem=xs.at[k], recv_sem=xr.at[k],
            device_id=(to, col), device_id_type=MESH)

    def y_copy(k):
        to = along_y + (k % 2) * (along_x - along_y)
        return pltpu.make_async_remote_copy(
            src_ref=first.at[k], dst_ref=second.at[k], send_sem=ys.at[k], recv_sem=yr.at[k],
            device_id=(to, col), device_id_type=MESH)

    def z_copy(src, k, to, sem):
        return pltpu.make_async_remote_copy(
            src_ref=src, dst_ref=left.at[core, k], send_sem=sem.at[k], recv_sem=zr.at[k],
            device_id=(row, to), device_id_type=MESH)

    def p_copy(src, k):
        return pltpu.make_async_remote_copy(
            src_ref=src, dst_ref=left.at[core, k], send_sem=ps.at[k], recv_sem=pr.at[k],
            device_id=(row, partner), device_id_type=MESH)

    go_up = jnp.logical_and(above >= 0, z < 3)
    go_down = jnp.logical_and(above <= 0, z > 0)

    def pass_on(src, k):
        @pl.when(go_up)
        def _():
            z_copy(src, k, col + 2, us).start()

        @pl.when(go_down)
        def _():
            z_copy(src, k, col - 2, ds).start()

        p_copy(src, k).start()

    @pl.loop(0, NCHUNK)
    def _(k):
        x_copy(k).start()

    load.wait()

    def out_copy(part, at):
        return pltpu.make_async_copy(
            acc.at[part, pl.ds(at, TILE), :], mult.at[part, pl.ds(at, TILE), :], out_sem.at[0])

    @pl.loop(0, NCHUNK + LAG + GROUP - 1)
    def _(s):
        @pl.when(s < NCHUNK)
        def _():
            x_copy(s).wait_recv()
            first[s] = first[s] + own[s]
            y_copy(s).start()

        k1 = s - 1

        @pl.when(jnp.logical_and(k1 >= 0, k1 < NCHUNK))
        def _():
            y_copy(k1).wait_recv()
            second[k1] = second[k1] + first[k1]

            @pl.when(above == 0)
            def _():
                pass_on(second.at[k1], k1)
                left[core, k1] = second[k1]

        k2 = s - 1 - far

        @pl.when(jnp.logical_and(far > 0, jnp.logical_and(k2 >= 0, k2 < NCHUNK)))
        def _():
            z_copy(second.at[k2], k2, partner, us).wait_recv()
            pass_on(left.at[core, k2], k2)

        k3 = s - LAG

        @pl.when(jnp.logical_and(k3 >= 0, k3 < NCHUNK))
        def _():
            pltpu.make_async_remote_copy(
                src_ref=second.at[k3], dst_ref=left.at[1 - core, k3], send_sem=ps.at[k3],
                recv_sem=pr.at[k3], device_id=(row, partner), device_id_type=MESH).wait_recv()

        step = s - (LAG + GROUP - 1)

        @pl.when(step >= 0)
        def _():
            group = step // GROUP
            part = step % GROUP

            @pl.when(part == 0)
            def _():
                re = second[pl.ds(group * GROUP, GROUP), 0]
                im = second[pl.ds(group * GROUP, GROUP), 1]
                right[0, :, 0] = re
                right[0, :, 1] = -im
                right[1, :, 0] = im
                right[1, :, 1] = re

            depth = 2 * GROUP * CHUNK
            per_half = width // TILE

            @pl.loop(0, 2 * per_half // GROUP)
            def _(i):
                tile = part * (2 * per_half // GROUP) + i
                half = tile // per_half
                inner = pl.multiple_of((tile % per_half) * TILE, TILE)
                at = pl.multiple_of(tile * TILE, TILE)
                lhs = left[half, pl.ds(group * GROUP, GROUP), :, :, pl.ds(inner, TILE)]
                lhs = lhs.reshape(depth, TILE)
                for c in range(2):
                    rhs = right[c].reshape(depth, width)
                    got = lax.dot_general(
                        lhs, rhs, (((0,), (0,)), ((), ())), preferred_element_type=jnp.float32)

                    @pl.when(group == 0)
                    def _():
                        acc[c, pl.ds(at, TILE), :] = got

                    @pl.when(group > 0)
                    def _():
                        acc[c, pl.ds(at, TILE), :] = acc[c, pl.ds(at, TILE), :] + got

                @pl.when(group == NGROUP - 1)
                def _():
                    for c in range(2):
                        out_copy(c, at).start()

    energy[...] = jnp.zeros_like(energy)

    @pl.loop(0, acc.shape[1] // 8)
    def _(i):
        at = pl.multiple_of(i * 8, 8)
        re = acc[0, pl.ds(at, 8), :]
        im = acc[1, pl.ds(at, 8), :]
        energy[...] = energy[...] + (re * re + im * im)

    pltpu.make_async_copy(acc, mult, out_sem.at[0]).wait()

    @pl.loop(0, NCHUNK)
    def _(k):
        x_copy(k).wait_send()
        y_copy(k).wait_send()
        p_copy(second.at[k], k).wait_send()

        @pl.when(go_up)
        def _():
            z_copy(second.at[k], k, col + 2, us).wait_send()

        @pl.when(go_down)
        def _():
            z_copy(second.at[k], k, col - 2, ds).wait_send()


def local_fast(wavefield, panel_order, filter_taps):
    shot_block = wavefield.shape[2]
    recv_block = wavefield.shape[3]
    factor = 1.0 / math.sqrt(STEPS * PANEL)
    count = 2.0 * SIDE * SIDE
    field = wavefield[:, 0]
    me = lax.axis_index("row")
    parts = []
    for t in range(STEPS):
        start = panel_order[t] * PANEL
        piece = lax.dynamic_slice_in_dim(field, start % shot_block, PANEL, 1)
        piece = jnp.where(me == start // shot_block, piece, jnp.zeros_like(piece))
        piece = piece.reshape(2, PANEL // CHUNK, CHUNK, recv_block)
        parts.append(jnp.swapaxes(piece, 0, 1))
    pieces = jnp.concatenate(parts, axis=0)
    block = (NCHUNK, 2, CHUNK, recv_block)
    dma = pltpu.SemaphoreType.DMA
    mult, energy = pl.pallas_call(
        predict_kernel,
        out_shape=(
            jax.ShapeDtypeStruct((2, shot_block, recv_block), jnp.float32),
            jax.ShapeDtypeStruct((8, recv_block), jnp.float32),
        ),
        in_specs=[pl.BlockSpec(memory_space=pl.ANY)],
        out_specs=(pl.BlockSpec(memory_space=pl.ANY), pl.BlockSpec(memory_space=pltpu.VMEM)),
        scratch_shapes=[
            pltpu.VMEM(block, jnp.bfloat16),
            pltpu.VMEM(block, jnp.bfloat16),
            pltpu.VMEM(block, jnp.bfloat16),
            pltpu.VMEM((2,) + block, jnp.bfloat16),
            pltpu.VMEM((2, shot_block, recv_block), jnp.float32),
            pltpu.VMEM((2, GROUP, 2, CHUNK, recv_block), jnp.bfloat16),
        ] + [dma((NCHUNK,))] * 9 + [dma, dma((1,))],
        compiler_params=pltpu.CompilerParams(
            collective_id=0, has_side_effects=True, vmem_limit_bytes=60 << 20),
        name="predict",
    )(pieces)
    local_data = jnp.sum(jnp.square(field.astype(jnp.float32)))
    both = jnp.stack([local_data, jnp.sum(energy) * (factor * factor)])
    both = lax.psum(both, ("row", "col"))
    gain = jnp.sqrt((both[0] / count + 1e-05) / (both[1] / count + 1e-05))
    spec_re, spec_im = frequency_spectrum(filter_taps, 1)
    mult_re = mult[0] * factor
    mult_im = mult[1] * factor
    sub_re = gain * (spec_re * mult_re - spec_im * mult_im)
    sub_im = gain * (spec_re * mult_im + spec_im * mult_re)
    out_re = (field[0].astype(jnp.float32) - sub_re).astype(jnp.bfloat16)
    out_im = (field[1].astype(jnp.float32) - sub_im).astype(jnp.bfloat16)
    return jnp.stack([out_re, out_im])[:, None]


def solution(mesh):
    in_specs = (P(None, None, "row", "col"), P(), P(None, "col"))
    out_specs = P(None, None, "row", "col")
    fast = mesh.shape["row"] == 4 and mesh.shape["col"] == 8
    body = local_fast if fast else local
    return jax.shard_map(body, mesh=mesh, in_specs=in_specs, out_specs=out_specs, check_vma=False)
```

```python
import math

import jax
import jax.numpy as jnp
from jax import lax
from jax.experimental import pallas as pl
from jax.experimental.pallas import tpu as pltpu
from jax.sharding import PartitionSpec as P

SIDE = 8192
PANEL = 512
STEPS = 3
TAPS = 11
FIRST_FREQUENCY = 8
NT = 1024
MESH = pl.DeviceIdType.MESH

CHUNK = 64
NCHUNK = STEPS * PANEL // CHUNK
GROUP = 256 // CHUNK
NGROUP = NCHUNK // GROUP
TILE = 256
HOP = 1
LAG = 5 * HOP
AHEAD = 2
STRIP = 64


def spread(block, axis, holder):
    block = jnp.where(lax.axis_index(axis) == holder, block, jnp.zeros_like(block))
    return lax.psum(block, axis)


def frequency_spectrum(filter_taps, freq_count):
    lags = jnp.arange(TAPS, dtype=jnp.float32)
    omega = 2.0 * math.pi * (FIRST_FREQUENCY + jnp.arange(freq_count, dtype=jnp.float32)) / NT
    phase = omega[:, None] * lags[None, :]
    real_part = jnp.dot(jnp.cos(phase), filter_taps, precision=lax.Precision.HIGHEST)
    imag_part = -jnp.dot(jnp.sin(phase), filter_taps, precision=lax.Precision.HIGHEST)
    return (real_part, imag_part)


def local(wavefield, panel_order, filter_taps):
    freq_count = wavefield.shape[1]
    shot_block = wavefield.shape[2]
    recv_block = wavefield.shape[3]
    own_row_index = lax.axis_index("row")
    factor = 1.0 / math.sqrt(STEPS * PANEL)
    count = 2.0 * SIDE * SIDE
    local_data = jnp.sum(jnp.square(wavefield.astype(jnp.float32)), axis=(0, 2, 3))
    energy_data = lax.psum(local_data, ("row", "col"))
    totals = jnp.zeros((freq_count, shot_block, 2 * recv_block), jnp.float32)
    for panel_advance in range(STEPS):
        first_point = panel_order[panel_advance] * PANEL
        row_width = min(PANEL, shot_block)
        owner_turn = 0
        start = first_point + owner_turn * row_width
        piece = lax.dynamic_slice_in_dim(wavefield, start % shot_block, row_width, 2)
        row_pieces = spread(piece, "row", start // shot_block)
        col_pieces = []
        mirror_width = min(shot_block, recv_block)
        for owner_turn in range(max(1, shot_block // recv_block)):
            start = own_row_index * shot_block + owner_turn * mirror_width
            piece = row_pieces
            col_pieces.append(spread(piece, "col", start // recv_block))
        upper = jnp.swapaxes(jnp.concatenate(col_pieces, axis=3), 2, 3)
        left_factor = jnp.concatenate([upper[0], upper[1]], axis=2)
        right_factor = jnp.concatenate(
            [
                jnp.concatenate([row_pieces[0], row_pieces[1]], axis=2),
                jnp.concatenate([-row_pieces[1], row_pieces[0]], axis=2),
            ],
            axis=1,
        )
        totals = totals + jnp.einsum(
            "yga,yah->ygh", left_factor, right_factor, preferred_element_type=jnp.float32
        )
    mult_re = totals[:, :, :recv_block] * factor
    mult_im = totals[:, :, recv_block:] * factor
    local_mult = jnp.sum(mult_re * mult_re, axis=(1, 2)) + jnp.sum(mult_im * mult_im, axis=(1, 2))
    energy_mult = lax.psum(local_mult, ("row", "col"))
    gain = jnp.sqrt((energy_data / count + 1e-05) / (energy_mult / count + 1e-05))[:, None, None]
    spec_re, spectrum_imaginary = frequency_spectrum(filter_taps, freq_count)
    a_re = spec_re[:, None, :]
    a_im = spectrum_imaginary[:, None, :]
    sub_re = gain * (a_re * mult_re - a_im * mult_im)
    subtracted_imaginary = gain * (a_re * mult_im + a_im * mult_re)
    result = jnp.stack(
        [
            wavefield[0].astype(jnp.float32) - sub_re,
            wavefield[1].astype(jnp.float32) - subtracted_imaginary,
        ]
    )
    return result.astype(jnp.bfloat16)


def predict_kernel(piece0, piece1, piece2, field, mult, gain,
                   own, first, second, left, acc, right, energy, strip, part_sums, row_sums, col_sums,
                   xs, xr, ys, yr, us, ds, zr, ps, pr, own_sem, out_sem, strip_sem,
                   rs, rr, cs, cr):
    panels = (piece0, piece1, piece2)
    per_panel = PANEL // CHUNK
    count = 2.0 * SIDE * SIDE
    factor = 1.0 / math.sqrt(STEPS * PANEL)
    row = lax.axis_index("row")
    col = lax.axis_index("col")
    z = col // 2
    core = col % 2
    along_x = row + 1 - 2 * (row % 2)
    along_y = (row + 2) % 4
    partner = col + 1 - 2 * core
    width = first.shape[3]
    above = z - row
    far = jnp.abs(above)

    loads = [
        pltpu.make_async_copy(panels[t], own.at[pl.ds(t * per_panel, per_panel)], own_sem.at[t])
        for t in range(STEPS)
    ]
    for load in loads:
        load.start()

    def strip_copy(s):
        return pltpu.make_async_copy(
            field.at[:, pl.ds(pl.multiple_of(s * STRIP, STRIP), STRIP), :],
            strip.at[s % 2], strip_sem.at[s % 2])

    nstrip = field.shape[1] // STRIP
    strip_copy(0).start()
    energy[...] = jnp.zeros_like(energy)
    barrier = pltpu.get_barrier_semaphore()
    for j in range(1, 4):
        pl.semaphore_signal(barrier, inc=1, device_id=((row + j) % 4, col), device_id_type=MESH)
    for j in range(1, 8):
        pl.semaphore_signal(barrier, inc=1, device_id=(row, (col + j) % 8), device_id_type=MESH)
    pl.semaphore_wait(barrier, 10)

    def x_copy(t, k):
        to = along_x + (k % 2) * (along_y - along_x)
        return pltpu.make_async_remote_copy(
            src_ref=panels[t].at[k - t * per_panel], dst_ref=first.at[k], send_sem=xs.at[k],
            recv_sem=xr.at[k], device_id=(to, col), device_id_type=MESH)

    def x_start(k):
        for t in range(STEPS):
            @pl.when(jnp.logical_and(k >= t * per_panel, k < (t + 1) * per_panel))
            def _():
                x_copy(t, k).start()

    def y_copy(k):
        to = along_y + (k % 2) * (along_x - along_y)
        return pltpu.make_async_remote_copy(
            src_ref=first.at[k], dst_ref=second.at[k], send_sem=ys.at[k], recv_sem=yr.at[k],
            device_id=(to, col), device_id_type=MESH)

    def z_copy(src, k, to, sem):
        return pltpu.make_async_remote_copy(
            src_ref=src, dst_ref=left.at[core, k], send_sem=sem.at[k], recv_sem=zr.at[k],
            device_id=(row, to), device_id_type=MESH)

    def p_copy(src, k):
        return pltpu.make_async_remote_copy(
            src_ref=src, dst_ref=left.at[core, k], send_sem=ps.at[k], recv_sem=pr.at[k],
            device_id=(row, partner), device_id_type=MESH)

    go_up = jnp.logical_and(above >= 0, z < 3)
    go_down = jnp.logical_and(above <= 0, z > 0)

    def pass_on(src, k):
        @pl.when(go_up)
        def _():
            z_copy(src, k, col + 2, us).start()

        @pl.when(go_down)
        def _():
            z_copy(src, k, col - 2, ds).start()

        p_copy(src, k).start()

    @pl.loop(0, AHEAD)
    def _(k):
        x_start(k)

    for load in loads:
        load.wait()

    def out_copy(part, at):
        return pltpu.make_async_copy(
            acc.at[part, pl.ds(at, TILE), :], mult.at[part, pl.ds(at, TILE), :], out_sem.at[0])

    @pl.loop(0, NCHUNK + LAG + GROUP - 1)
    def _(s):
        @pl.when(s < NCHUNK)
        def _():
            x_start(s + AHEAD)
            arrival = pltpu.make_async_remote_copy(
                src_ref=second.at[s], dst_ref=first.at[s], send_sem=xs.at[s], recv_sem=xr.at[s],
                device_id=(along_x, col), device_id_type=MESH)
            arrival.wait_recv()
            first[s] = first[s] + own[s]
            y_copy(s).start()

        k1 = s - HOP

        @pl.when(jnp.logical_and(k1 >= 0, k1 < NCHUNK))
        def _():
            y_copy(k1).wait_recv()
            second[k1] = second[k1] + first[k1]

            @pl.when(above == 0)
            def _():
                pass_on(second.at[k1], k1)
                left[core, k1] = second[k1]

        k2 = s - HOP * (1 + far)

        @pl.when(jnp.logical_and(far > 0, jnp.logical_and(k2 >= 0, k2 < NCHUNK)))
        def _():
            z_copy(second.at[k2], k2, partner, us).wait_recv()
            pass_on(left.at[core, k2], k2)

        k3 = s - LAG

        @pl.when(jnp.logical_and(k3 >= 0, k3 < NCHUNK))
        def _():
            pltpu.make_async_remote_copy(
                src_ref=second.at[k3], dst_ref=left.at[1 - core, k3], send_sem=ps.at[k3],
                recv_sem=pr.at[k3], device_id=(row, partner), device_id_type=MESH).wait_recv()

        @pl.when(s < nstrip)
        def _():
            strip_copy(s).wait()

            @pl.when(s + 1 < nstrip)
            def _():
                strip_copy(s + 1).start()

            value = strip[s % 2].astype(jnp.float32)
            energy[0] = energy[0] + jnp.sum((value * value).reshape(2 * STRIP // 8, 8, width), axis=0)

        step = s - (LAG + GROUP - 1)

        @pl.when(step >= 0)
        def _():
            group = step // GROUP
            part = step % GROUP

            @pl.when(part == 0)
            def _():
                re = second[pl.ds(group * GROUP, GROUP), 0]
                im = second[pl.ds(group * GROUP, GROUP), 1]
                right[0, :, 0] = re
                right[0, :, 1] = -im
                right[1, :, 0] = im
                right[1, :, 1] = re

            depth = 2 * GROUP * CHUNK
            per_half = width // TILE

            @pl.loop(0, 2 * per_half // GROUP)
            def _(i):
                tile = part * (2 * per_half // GROUP) + i
                half = tile // per_half
                inner = pl.multiple_of((tile % per_half) * TILE, TILE)
                at = pl.multiple_of(tile * TILE, TILE)
                lhs = left[half, pl.ds(group * GROUP, GROUP), :, :, pl.ds(inner, TILE)]
                lhs = lhs.reshape(depth, TILE)
                for c in range(2):
                    rhs = right[c].reshape(depth, width)
                    got = lax.dot_general(
                        lhs, rhs, (((0,), (0,)), ((), ())), preferred_element_type=jnp.float32)

                    @pl.when(group == 0)
                    def _():
                        acc[c, pl.ds(at, TILE), :] = got

                    @pl.when(jnp.logical_and(group > 0, group < NGROUP - 1))
                    def _():
                        acc[c, pl.ds(at, TILE), :] = acc[c, pl.ds(at, TILE), :] + got

                    @pl.when(group == NGROUP - 1)
                    def _():
                        value = (acc[c, pl.ds(at, TILE), :] + got) * factor
                        acc[c, pl.ds(at, TILE), :] = value
                        energy[1] = energy[1] + jnp.sum(
                            (value * value).reshape(TILE // 8, 8, width), axis=0)

                @pl.when(group == NGROUP - 1)
                def _():
                    for c in range(2):
                        out_copy(c, at).start()

    sums = energy[:, :, :128]
    for j in range(1, width // 128):
        sums = sums + energy[:, :, j * 128:(j + 1) * 128]
    part_sums[0] = sums

    @pl.loop(0, NCHUNK)
    def _(k):
        pltpu.make_async_remote_copy(
            src_ref=own.at[k], dst_ref=first.at[k], send_sem=xs.at[k], recv_sem=xr.at[k],
            device_id=(along_x, col), device_id_type=MESH).wait_send()
        y_copy(k).wait_send()
        p_copy(second.at[k], k).wait_send()

        @pl.when(go_up)
        def _():
            z_copy(second.at[k], k, col + 2, us).wait_send()

        @pl.when(go_down)
        def _():
            z_copy(second.at[k], k, col - 2, ds).wait_send()

    row_copies = [
        pltpu.make_async_remote_copy(
            src_ref=part_sums.at[0], dst_ref=row_sums.at[j - 1], send_sem=rs.at[j - 1],
            recv_sem=rr.at[j - 1], device_id=((row + j) % 4, col), device_id_type=MESH)
        for j in range(1, 4)
    ]
    for copy in row_copies:
        copy.start()
    for j in range(3):
        row_copies[j].wait_recv()
        sums = sums + row_sums[j]
    part_sums[1] = sums
    col_copies = [
        pltpu.make_async_remote_copy(
            src_ref=part_sums.at[1], dst_ref=col_sums.at[j - 1], send_sem=cs.at[j - 1],
            recv_sem=cr.at[j - 1], device_id=(row, (col + j) % 8), device_id_type=MESH)
        for j in range(1, 8)
    ]
    pltpu.make_async_copy(acc, mult, out_sem.at[0]).wait()
    for copy in col_copies:
        copy.start()
    for j in range(7):
        col_copies[j].wait_recv()
        sums = sums + col_sums[j]
    data = jnp.full((8, 128), jnp.sum(sums[0]), jnp.float32)
    predicted = jnp.full((8, 128), jnp.sum(sums[1]), jnp.float32)
    gain[...] = jnp.sqrt((data / count + 1e-05) / (predicted / count + 1e-05))
    for copy in row_copies + col_copies:
        copy.wait_send()


def local_fast(wavefield, panel_order, filter_taps):
    shot_block = wavefield.shape[2]
    recv_block = wavefield.shape[3]
    field = wavefield[:, 0]
    me = lax.axis_index("row")
    parts = []
    for t in range(STEPS):
        start = panel_order[t] * PANEL
        piece = lax.dynamic_slice_in_dim(field, start % shot_block, PANEL, 1)
        piece = jnp.where(me == start // shot_block, piece, jnp.zeros_like(piece))
        piece = piece.reshape(2, PANEL // CHUNK, CHUNK, recv_block)
        parts.append(jnp.swapaxes(piece, 0, 1))
    block = (NCHUNK, 2, CHUNK, recv_block)
    dma = pltpu.SemaphoreType.DMA
    mult, gain = pl.pallas_call(
        predict_kernel,
        out_shape=(
            jax.ShapeDtypeStruct((2, shot_block, recv_block), jnp.float32),
            jax.ShapeDtypeStruct((8, 128), jnp.float32),
        ),
        in_specs=[pl.BlockSpec(memory_space=pl.ANY)] * 4,
        out_specs=(pl.BlockSpec(memory_space=pl.ANY), pl.BlockSpec(memory_space=pltpu.VMEM)),
        scratch_shapes=[
            pltpu.VMEM(block, jnp.bfloat16),
            pltpu.VMEM(block, jnp.bfloat16),
            pltpu.VMEM(block, jnp.bfloat16),
            pltpu.VMEM((2,) + block, jnp.bfloat16),
            pltpu.VMEM((2, shot_block, recv_block), jnp.float32),
            pltpu.VMEM((2, GROUP, 2, CHUNK, recv_block), jnp.bfloat16),
            pltpu.VMEM((2, 8, recv_block), jnp.float32),
            pltpu.VMEM((2, 2, STRIP, recv_block), jnp.bfloat16),
            pltpu.VMEM((2, 2, 8, 128), jnp.float32),
            pltpu.VMEM((3, 2, 8, 128), jnp.float32),
            pltpu.VMEM((7, 2, 8, 128), jnp.float32),
        ] + [dma((NCHUNK,))] * 9 + [
            dma((STEPS,)), dma((1,)), dma((2,)), dma((3,)), dma((3,)), dma((7,)), dma((7,))],
        compiler_params=pltpu.CompilerParams(
            collective_id=0, has_side_effects=True, vmem_limit_bytes=60 << 20),
        name="predict",
    )(*parts, field)
    scale = gain[0, 0]
    spec_re, spec_im = frequency_spectrum(filter_taps, 1)
    same = jnp.stack([spec_re, spec_re])
    cross = jnp.stack([-spec_im, spec_im])
    moved = scale * (same * mult + cross * mult[::-1])
    return (field.astype(jnp.float32) - moved).astype(jnp.bfloat16)[:, None]


def solution(mesh):
    in_specs = (P(None, None, "row", "col"), P(), P(None, "col"))
    out_specs = P(None, None, "row", "col")
    fast = mesh.shape["row"] == 4 and mesh.shape["col"] == 8
    body = local_fast if fast else local
    return jax.shard_map(body, mesh=mesh, in_specs=in_specs, out_specs=out_specs, check_vma=False)
```
